32 devices in a mesh: groups: 2 (over y), feat: 4 (over z), dp: 2 (over x), rep: 2 (over core).
Axes of the slice: x: 2, y: 2, z: 4, core: 2. Of those that a mesh axis runs over, the one named last changes fastest.
Arguments:
- tokens: bfloat16 [4096, 16384], P(('groups', 'dp', 'rep'), 'feat'), parts along dimension 0, may hold values from -6 to 6
- cotangent: bfloat16 [4096, 16384], P(('groups', 'dp', 'rep'), 'feat'), parts along dimension 0, may hold values from -6 to 6
- mix_first: bfloat16 [128, 2, 128, 128], P('feat'), may hold values from -0.375 to 0.375
- up_weight: bfloat16 [128, 128, 512], P('feat'), may hold values from -0.5 to 0.5
- down_weight: bfloat16 [128, 512, 128], P('feat'), may hold values from -0.25 to 0.25
- mix_second: bfloat16 [128, 2, 128, 128], P('feat'), may hold values from -0.375 to 0.375
- order: int32 [128], P('feat'), may hold values from 0 to 31, as said below
Outputs:
- grad_tokens: bfloat16 [4096, 16384], P(('groups', 'dp', 'rep'), 'feat'), parts along dimension 0
- grad_first: float32 [256, 2, 128, 128], P(('groups', 'feat'), None, ('dp', 'rep')), parts along dimension 0
- grad_up: float32 [256, 128, 512], P(('groups', 'feat'), ('dp', 'rep')), parts along dimension 0
- grad_down: float32 [256, 512, 128], P(('groups', 'feat'), ('dp', 'rep')), parts along dimension 0
- grad_second: float32 [256, 2, 128, 128], P(('groups', 'feat'), None, ('dp', 'rep')), parts along dimension 0
The draws below stay inside these ranges and needn't reach their ends.
There are 2 independent parts, one for each index of `groups`. The reference program is written for one: setup_inputs(seed, part) draws one part's arguments, and reference() takes and returns one part's arrays. A program takes and returns all parts, laid end to end along the dimension named above; an argument that names none is the same for every part. Nothing has to cross between parts.
Inputs may be any that keep to these rules, and one draw needn't show every extreme that they name: `order`: each aligned run of 32 entries (the blocks of one index of feat) is a permutation of 0 to 31.
All inputs are finite; a program needn't handle non-finite values.
Results may differ from the reference program's by a relative error of at most 0.0095.
Values may be sent and summed in bfloat16 or wider, within the bound.
A program may use at most 256 MiB of HBM per device.

```python
import jax
import jax.numpy as jnp
from jax import lax

D = 16384
BS = 128
BLOCKS = 128
BLOCKS_DEV = 32
HB = 512
TOKENS = 2048
N_DP = 2
N_REP = 2


def draw_order(key, part):
    subkeys = jax.random.split(key, BLOCKS // BLOCKS_DEV)

    def shuffle_run(subkey):
        return jax.random.permutation(subkey, BLOCKS_DEV)
    shuffled = jax.vmap(shuffle_run)(subkeys)
    return shuffled.reshape(BLOCKS).astype(jnp.int32)


def steps_of(stream_key, dims, shards, least, high):
    factor_of = 1.0
    for position, shards_of in shards:
        steps = jax.random.uniform(jax.random.fold_in(jax.random.fold_in(stream_key, 6), position), (shards_of,), jnp.float32, least / len(shards), high / len(shards))
        factor_of = factor_of * jnp.repeat(jnp.exp(steps), dims[position] // shards_of).reshape((-1,) + (1,) * (len(dims) - 1 - position))
    return factor_of


def centred(stream_key, dims, scale, limit, cuts=(), held_as=jnp.bfloat16):
    drawn = jax.random.normal(stream_key, dims, jnp.float32) * scale
    if len(cuts) > 0:
        drawn = steps_of(stream_key, dims, cuts, -0.22, 0.18) * drawn
    return jnp.clip(drawn, min=-limit, max=limit).astype(held_as)


def setup_inputs(seed: int = 0, part: int = 0) -> dict:
    arg_keys = jax.random.split(jax.random.key(seed), 8)
    own_keys = jax.random.split(jax.random.fold_in(arg_keys[7], part), 8)
    tokens = centred(own_keys[0], (TOKENS, D), 1.0, 6.0, ((0, 4), (1, 4)))
    cotangent = centred(own_keys[1], (TOKENS, D), 1.0, 6.0, ((0, 4), (1, 4)))
    mix_first = centred(arg_keys[2], (BLOCKS, 2, BS, BS), (2 * BS) ** -0.5, 0.375, ((0, 4),))
    up_weight = centred(arg_keys[3], (BLOCKS, BS, HB), BS ** -0.5, 0.5, ((0, 4),))
    down_weight = centred(arg_keys[4], (BLOCKS, HB, BS), HB ** -0.5, 0.25, ((0, 4),))
    mix_second = centred(arg_keys[5], (BLOCKS, 2, BS, BS), (2 * BS) ** -0.5, 0.375, ((0, 4),))
    order = draw_order(jax.random.fold_in(arg_keys[7], 71), part)
    return {"tokens": tokens, "cotangent": cotangent, "mix_first": mix_first, "up_weight": up_weight, "down_weight": down_weight, "mix_second": mix_second, "order": order}


GELU_C = 0.7978845608028654
GELU_K = 0.044715


def gelu_value(hidden):
    tanh_input = GELU_C * (hidden + GELU_K * hidden * hidden * hidden)
    return 0.5 * hidden * (1.0 + jnp.tanh(tanh_input))


def gelu_slope(hidden):
    tanh_input = GELU_C * (hidden + GELU_K * hidden * hidden * hidden)
    tangent = jnp.tanh(tanh_input)
    return 0.5 * (1.0 + tangent) + 0.5 * hidden * (1.0 - tangent * tangent) * GELU_C * (1.0 + 3.0 * GELU_K * hidden * hidden)


def forward_mix(direct, weights):
    return jnp.einsum("tbi,bij->tbj", direct.astype(jnp.float32), weights.astype(jnp.float32))


def backward_mix(direct, weights):
    return jnp.einsum("tbj,bij->tbi", direct.astype(jnp.float32), weights.astype(jnp.float32))


def group_blocks(left, right):
    groups = N_DP * N_REP
    left_groups = left.astype(jnp.float32).reshape(groups, TOKENS // groups, left.shape[1], left.shape[2])
    right_groups = right.astype(jnp.float32).reshape(groups, TOKENS // groups, right.shape[1], right.shape[2])
    partial_terms = jnp.einsum("gtbi,gtbj->gbij", left_groups, right_groups)
    return jnp.sum(partial_terms.astype(jnp.bfloat16).astype(jnp.float32), axis=0)


def group_pair(left, right):
    groups = N_DP * N_REP
    left_groups = left.astype(jnp.float32).reshape(groups, TOKENS // groups, left.shape[1])
    right_groups = right.astype(jnp.float32).reshape(groups, TOKENS // groups, right.shape[1])
    partial_terms = jnp.einsum("gti,gtj->gij", left_groups, right_groups)
    return jnp.sum(partial_terms.astype(jnp.bfloat16).astype(jnp.float32), axis=0)


def forward_block(operands):
    block_in, block_up, block_down = operands
    hidden_pre = jnp.dot(block_in, block_up, preferred_element_type=jnp.float32)
    activated = gelu_value(hidden_pre).astype(jnp.bfloat16)
    return jnp.dot(activated, block_down, preferred_element_type=jnp.float32).astype(jnp.bfloat16)


def backward_block(operands):
    block_in, block_grad, block_up, block_down = operands
    hidden_pre = jnp.dot(block_in, block_up, preferred_element_type=jnp.float32)
    activated = gelu_value(hidden_pre).astype(jnp.bfloat16)
    grad_down = group_pair(activated, block_grad)
    grad_act = jnp.dot(block_grad, block_down.T, preferred_element_type=jnp.float32)
    grad_pre = (grad_act * gelu_slope(hidden_pre)).astype(jnp.bfloat16)
    grad_up = group_pair(block_in, grad_pre)
    grad_in = jnp.dot(grad_pre, block_up.T, preferred_element_type=jnp.float32).astype(jnp.bfloat16)
    return grad_down, grad_up, grad_in


def reference(tokens, cotangent, mix_first, up_weight, down_weight, mix_second, order):
    block_ids = jnp.arange(BLOCKS, dtype=jnp.int32)
    far_index = jnp.bitwise_xor(block_ids, BLOCKS // 2).astype(jnp.int32)
    near_index = jnp.bitwise_xor(block_ids, BLOCKS_DEV).astype(jnp.int32)
    source = ((block_ids // BLOCKS_DEV) * BLOCKS_DEV + order).astype(jnp.int32)
    inputs = tokens.reshape(TOKENS, BLOCKS, BS)
    upstream = cotangent.reshape(TOKENS, BLOCKS, BS)
    partner_in = inputs[:, far_index]
    mixed = (forward_mix(inputs, mix_first[:, 0]) + forward_mix(partner_in, mix_first[:, 1])).astype(jnp.bfloat16)
    permuted = mixed[:, source]
    block_major = jnp.swapaxes(permuted, 0, 1)
    reduced = jnp.swapaxes(lax.map(forward_block, (block_major, up_weight, down_weight)), 0, 1)
    partner_out = reduced[:, near_index]
    grad_second = jnp.stack([group_blocks(reduced, upstream), group_blocks(partner_out, upstream)], axis=1)
    partner_term = backward_mix(upstream, mix_second[:, 1]).astype(jnp.bfloat16)
    grad_reduced = (backward_mix(upstream, mix_second[:, 0]) + partner_term[:, near_index].astype(jnp.float32)).astype(jnp.bfloat16)
    grad_down, grad_up, grad_perm = lax.map(backward_block, (block_major, jnp.swapaxes(grad_reduced, 0, 1), up_weight, down_weight))
    grad_perm = jnp.swapaxes(grad_perm, 0, 1)
    grad_mixed = jnp.zeros_like(grad_perm).at[:, source].set(grad_perm)
    back_term = backward_mix(grad_mixed, mix_first[:, 1]).astype(jnp.bfloat16)
    grad_inputs = (backward_mix(grad_mixed, mix_first[:, 0]) + back_term[:, far_index].astype(jnp.float32)).astype(jnp.bfloat16)
    grad_first = jnp.stack([group_blocks(inputs, grad_mixed), group_blocks(partner_in, grad_mixed)], axis=1)
    return grad_inputs.reshape(TOKENS, D), grad_first, grad_up, grad_down, grad_second
```

```python
import functools

import jax
import jax.numpy as jnp
from jax import lax
from jax.experimental import pallas as pl
from jax.experimental.pallas import tpu as pltpu
from jax.sharding import PartitionSpec as P

GELU_C = 0.7978845608028654
GELU_K = 0.044715
CHUNKS = 2


def swapped(x, axis, bit):
    return lax.ppermute(x, axis, [(i, i ^ 1 << bit) for i in range(lax.axis_size(axis))])


def dot(left, right, dims):
    return lax.dot_general(left, right, (dims, ((), ())), preferred_element_type=jnp.float32)


NN = ((1,), (0,))
NT = ((1,), (1,))
TN = ((0,), (0,))


def block_kernel(has_prev, order_ref, x_ref, xf_ref, c_ref, cn_ref, mix_ref, up_ref, down_ref, p_ref, q_ref, *rest):
    if has_prev:
        prev, rest = rest[:4], rest[4:]
    else:
        prev = None
    r_ref, dx_ref, gf_ref, gu_ref, gd_ref, gs_ref = rest
    width = x_ref.shape[1]

    def emit(ref, which, value, index):
        if prev is not None:
            value = value + prev[which][index].astype(jnp.float32)
        ref[index] = value.astype(ref.dtype)

    x2 = jnp.concatenate([x_ref[...], xf_ref[...]], axis=1)
    c2 = jnp.concatenate([c_ref[...], cn_ref[...]], axis=1)
    mix = mix_ref[0].reshape(2 * width, width)
    pq = jnp.concatenate([p_ref[0, 0], q_ref[0]], axis=1)
    up = up_ref[0]
    down = down_ref[0]
    v = dot(x2, mix, NN).astype(jnp.bfloat16)
    dz = dot(c2, pq, NT).astype(jnp.bfloat16)
    h = dot(v, up, NN)
    da = dot(dz, down, NT)
    h2 = h * h
    t = jnp.tanh(h * (GELU_C + (GELU_C * GELU_K) * h2))
    p = 0.5 + 0.5 * t
    act = h * p
    slope = p + act * (1.0 - p) * (2.0 * GELU_C + (6.0 * GELU_C * GELU_K) * h2)
    a = act.astype(jnp.bfloat16)
    dh = (da * slope).astype(jnp.bfloat16)
    z = dot(a, down, NN).astype(jnp.bfloat16)
    du = dot(dh, up, NT).astype(jnp.bfloat16)
    both = dot(du, mix, NT)
    dx_ref[...] = both[:, :width]
    r_ref[...] = both[:, width:].astype(jnp.bfloat16)
    gf = dot(x2, du, TN)
    emit(gf_ref, 0, gf[:width], (0, 0))
    emit(gf_ref, 0, gf[width:], (0, 1))
    emit(gu_ref, 1, dot(v, dh, TN), 0)
    emit(gd_ref, 2, dot(a, dz, TN), 0)
    gs = dot(z, c2, TN)
    emit(gs_ref, 3, gs[:, :width], (0, 0))
    emit(gs_ref, 3, gs[:, width:], (0, 1))


def process(chunk, rows, order, tokens, far_in, cotangent, near_in, mix_first, up, down, mix_second, near_q, prev):
    blocks, _, width, _ = mix_first.shape
    hidden = up.shape[2]
    at_source = lambda b, o: (0, o[b])
    act_spec = lambda m: pl.BlockSpec((rows, width), m)
    first_spec = pl.BlockSpec((1, 2, width, width), lambda b, o: (o[b], 0, 0, 0))
    up_spec = pl.BlockSpec((1, width, hidden), lambda b, o: (b, 0, 0))
    down_spec = pl.BlockSpec((1, hidden, width), lambda b, o: (b, 0, 0))
    second_spec = pl.BlockSpec((1, 2, width, width), lambda b, o: (b, 0, 0, 0))
    grad_specs = [first_spec, up_spec, down_spec, second_spec]
    in_specs = [
        act_spec(lambda b, o: (chunk, o[b])),
        act_spec(at_source),
        act_spec(lambda b, o: (chunk, b)),
        act_spec(lambda b, o: (0, b)),
        first_spec,
        up_spec,
        down_spec,
        pl.BlockSpec((1, 1, width, width), lambda b, o: (b, 0, 0, 0)),
        pl.BlockSpec((1, width, width), lambda b, o: (b, 0, 0)),
    ]
    operands = [tokens, far_in, cotangent, near_in, mix_first, up, down, mix_second, near_q]
    if prev is not None:
        in_specs += grad_specs
        operands += prev
    bf = jnp.bfloat16
    out_shape = [
        jax.ShapeDtypeStruct((rows, blocks * width), bf),
        jax.ShapeDtypeStruct((rows, blocks * width), jnp.float32),
        jax.ShapeDtypeStruct(mix_first.shape, bf),
        jax.ShapeDtypeStruct(up.shape, bf),
        jax.ShapeDtypeStruct(down.shape, bf),
        jax.ShapeDtypeStruct(mix_second.shape, bf),
    ]
    macs = rows * blocks * width * (10 * width + 6 * hidden)
    out = pl.pallas_call(
        functools.partial(block_kernel, prev is not None),
        grid_spec=pltpu.PrefetchScalarGridSpec(
            num_scalar_prefetch=1,
            grid=(blocks,),
            in_specs=in_specs,
            out_specs=[act_spec(at_source), act_spec(at_source)] + grad_specs,
        ),
        out_shape=out_shape,
        compiler_params=pltpu.CompilerParams(dimension_semantics=("arbitrary",)),
        cost_estimate=pl.CostEstimate(
            flops=4 * macs,
            bytes_accessed=60 * 2**20,
            transcendentals=rows * blocks * hidden,
        ),
        name=f"blocks{chunk}",
    )(order, *operands)
    return out[0], out[1], list(out[2:])


def summed(parts, row_dim):
    stages = [("rep", bit) for bit in range(lax.axis_size("rep").bit_length() - 1)]
    dp_bits = lax.axis_size("dp").bit_length() - 1
    rep_bits = len(stages)
    stages += [("dp", bit) for bit in reversed(range(dp_bits))]
    shape = parts.shape
    owners = 1 << (dp_bits + rep_bits)
    names = [("dp", bit) for bit in reversed(range(dp_bits))]
    names += [("rep", bit) for bit in reversed(range(rep_bits))]
    x = parts.reshape(
        shape[:row_dim] + (2,) * len(names) + (shape[row_dim] // owners,) + shape[row_dim + 1 :]
    )
    for axis, bit in stages:
        where = row_dim + names.index((axis, bit))
        names.remove((axis, bit))
        mine = (lax.axis_index(axis) >> bit) & 1
        kept = lax.dynamic_index_in_dim(x, mine, where, keepdims=False)
        sent = lax.dynamic_index_in_dim(x, 1 - mine, where, keepdims=False)
        got = swapped(sent, axis, bit)
        x = kept.astype(jnp.float32) + got.astype(jnp.float32)
        if names:
            x = x.astype(jnp.bfloat16)
    return x


def per_device(tokens, cotangent, mix_first, up_weight, down_weight, mix_second, order):
    row_count = tokens.shape[0]
    top_bit = lax.axis_size("feat").bit_length() - 2
    rows = row_count // CHUNKS
    cut = lambda x, i: lax.slice_in_dim(x, i * rows, (i + 1) * rows, axis=0)
    far_in, near_in = [], []
    near_q = None
    for i in range(CHUNKS):
        far_in.append(swapped(cut(tokens, i), "feat", top_bit))
        if i == 0:
            near_q = swapped(mix_second[:, 1], "feat", 0)
        near_in.append(swapped(cut(cotangent, i), "feat", 0))
    grads = None
    backs, directs = [], []
    for i in range(CHUNKS):
        back, direct, grads = process(
            i, rows, order, tokens, far_in[i], cotangent, near_in[i],
            mix_first, up_weight, down_weight, mix_second, near_q, grads,
        )
        backs.append(swapped(back, "feat", top_bit))
        directs.append(direct)
    first, up, down, second = grads
    second_sum = summed(second, 2)
    near_sum = swapped(second_sum[:, 1].astype(jnp.bfloat16), "feat", 0).astype(jnp.float32)
    second_sum = jnp.stack([second_sum[:, 0], near_sum], axis=1)
    up_sum = summed(up, 1)
    down_sum = summed(down, 1)
    first_sum = summed(first, 2)
    grad_inputs = jnp.concatenate(
        [
            (direct + back.astype(jnp.float32)).astype(jnp.bfloat16)
            for direct, back in zip(directs, backs)
        ],
        axis=0,
    )
    return grad_inputs, first_sum, up_sum, down_sum, second_sum


def solution(mesh):
    placed = (
        P(("groups", "dp", "rep"), "feat"),
        P(("groups", "dp", "rep"), "feat"),
        P("feat", None, None, None),
        P("feat", None, None),
        P("feat", None, None),
        P("feat", None, None, None),
        P("feat"),
    )
    return jax.shard_map(
        per_device,
        mesh=mesh,
        in_specs=placed,
        out_specs=(
            P(("groups", "dp", "rep"), "feat"),
            P(("groups", "feat"), None, ("dp", "rep"), None),
            P(("groups", "feat"), ("dp", "rep"), None),
            P(("groups", "feat"), ("dp", "rep"), None),
            P(("groups", "feat"), None, ("dp", "rep"), None),
        ),
        check_vma=False,
    )
```

```python
import functools

import jax
import jax.numpy as jnp
from jax import lax
from jax.experimental import pallas as pl
from jax.experimental.pallas import tpu as pltpu
from jax.sharding import PartitionSpec as P


GELU_C = 0.7978845608028654
GELU_K = 0.044715
SHARES = (1, 1, 2)


def swapped(x, axis, bit):
    return lax.ppermute(x, axis, [(i, i ^ 1 << bit) for i in range(lax.axis_size(axis))])


def dot(left, right, dims):
    return lax.dot_general(left, right, (dims, ((), ())), preferred_element_type=jnp.float32)


NN = ((1,), (0,))
NT = ((1,), (1,))
TN = ((0,), (0,))


def block_kernel(has_prev, order_ref, x_ref, xf_ref, c_ref, cn_ref, mix_ref, up_ref, down_ref, p_ref, q_ref, *rest):
    if has_prev:
        prev, rest = rest[:4], rest[4:]
    else:
        prev = None
    r_ref, dx_ref, gf_ref, gu_ref, gd_ref, gs_ref = rest
    width = x_ref.shape[1]

    def emit(ref, which, value, index):
        if prev is not None:
            value = value + prev[which][index].astype(jnp.float32)
        ref[index] = value.astype(ref.dtype)

    x2 = jnp.concatenate([x_ref[...], xf_ref[...]], axis=1)
    c2 = jnp.concatenate([c_ref[...], cn_ref[...]], axis=1)
    mix = mix_ref[0].reshape(2 * width, width)
    pq = jnp.concatenate([p_ref[0, 0], q_ref[0]], axis=1)
    up = up_ref[0]
    down = down_ref[0]
    v = dot(x2, mix, NN).astype(jnp.bfloat16)
    dz = dot(c2, pq, NT).astype(jnp.bfloat16)
    h = dot(v, up, NN)
    da = dot(dz, down, NT)
    h2 = h * h
    t = jnp.tanh(h * (GELU_C + (GELU_C * GELU_K) * h2))
    p = 0.5 + 0.5 * t
    act = h * p
    slope = p + act * (1.0 - p) * (2.0 * GELU_C + (6.0 * GELU_C * GELU_K) * h2)
    a = act.astype(jnp.bfloat16)
    dh = (da * slope).astype(jnp.bfloat16)
    z = dot(a, down, NN).astype(jnp.bfloat16)
    du = dot(dh, up, NT).astype(jnp.bfloat16)
    both = dot(du, mix, NT)
    dx_ref[...] = both[:, :width]
    r_ref[...] = both[:, width:].astype(jnp.bfloat16)
    gf = dot(x2, du, TN)
    emit(gf_ref, 0, gf[:width], (0, 0))
    emit(gf_ref, 0, gf[width:], (0, 1))
    emit(gu_ref, 1, dot(v, dh, TN), 0)
    emit(gd_ref, 2, dot(a, dz, TN), 0)
    gs = dot(z, c2, TN)
    emit(gs_ref, 3, gs[:, :width], (0, 0))
    emit(gs_ref, 3, gs[:, width:], (0, 1))


def process(offset, rows, order, tokens, far_in, cotangent, near_in, mix_first, up, down, mix_second, near_q, prev):
    blocks, _, width, _ = mix_first.shape
    hidden = up.shape[2]
    at_source = lambda b, o: (0, o[b])
    act_spec = lambda m: pl.BlockSpec((rows, width), m)
    first_spec = pl.BlockSpec((1, 2, width, width), lambda b, o: (o[b], 0, 0, 0))
    up_spec = pl.BlockSpec((1, width, hidden), lambda b, o: (b, 0, 0))
    down_spec = pl.BlockSpec((1, hidden, width), lambda b, o: (b, 0, 0))
    second_spec = pl.BlockSpec((1, 2, width, width), lambda b, o: (b, 0, 0, 0))
    grad_specs = [first_spec, up_spec, down_spec, second_spec]
    in_specs = [
        act_spec(lambda b, o: (offset // rows, o[b])),
        act_spec(at_source),
        act_spec(lambda b, o: (offset // rows, b)),
        act_spec(lambda b, o: (0, b)),
        first_spec,
        up_spec,
        down_spec,
        pl.BlockSpec((1, 1, width, width), lambda b, o: (b, 0, 0, 0)),
        pl.BlockSpec((1, width, width), lambda b, o: (b, 0, 0)),
    ]
    operands = [tokens, far_in, cotangent, near_in, mix_first, up, down, mix_second, near_q]
    if prev is not None:
        in_specs += grad_specs
        operands += prev
    bf = jnp.bfloat16
    out_shape = [
        jax.ShapeDtypeStruct((rows, blocks * width), bf),
        jax.ShapeDtypeStruct((rows, blocks * width), jnp.float32),
        jax.ShapeDtypeStruct(mix_first.shape, bf),
        jax.ShapeDtypeStruct(up.shape, bf),
        jax.ShapeDtypeStruct(down.shape, bf),
        jax.ShapeDtypeStruct(mix_second.shape, bf),
    ]
    macs = rows * blocks * width * (10 * width + 6 * hidden)
    out = pl.pallas_call(
        functools.partial(block_kernel, prev is not None),
        grid_spec=pltpu.PrefetchScalarGridSpec(
            num_scalar_prefetch=1,
            grid=(blocks,),
            in_specs=in_specs,
            out_specs=[act_spec(at_source), act_spec(at_source)] + grad_specs,
        ),
        out_shape=out_shape,
        compiler_params=pltpu.CompilerParams(dimension_semantics=("arbitrary",)),
        cost_estimate=pl.CostEstimate(
            flops=4 * macs,
            bytes_accessed=60 * 2**20,
            transcendentals=rows * blocks * hidden,
        ),
    )(order, *operands)
    return out[0], out[1], list(out[2:])


def summed(parts, row_dim):
    stages = [("rep", bit) for bit in range(lax.axis_size("rep").bit_length() - 1)]
    dp_bits = lax.axis_size("dp").bit_length() - 1
    rep_bits = len(stages)
    stages += [("dp", bit) for bit in reversed(range(dp_bits))]
    shape = parts.shape
    owners = 1 << (dp_bits + rep_bits)
    names = [("dp", bit) for bit in reversed(range(dp_bits))]
    names += [("rep", bit) for bit in reversed(range(rep_bits))]
    x = parts.reshape(
        shape[:row_dim] + (2,) * len(names) + (shape[row_dim] // owners,) + shape[row_dim + 1 :]
    )
    for axis, bit in stages:
        where = row_dim + names.index((axis, bit))
        names.remove((axis, bit))
        mine = (lax.axis_index(axis) >> bit) & 1
        kept = lax.dynamic_index_in_dim(x, mine, where, keepdims=False)
        sent = lax.dynamic_index_in_dim(x, 1 - mine, where, keepdims=False)
        got = swapped(sent, axis, bit)
        x = kept.astype(jnp.float32) + got.astype(jnp.float32)
        if names:
            x = x.astype(jnp.bfloat16)
    return x


def neighbour_weights(weights):
    half = weights.shape[0] // 2
    side = lax.axis_index("rep")
    part = lax.dynamic_slice_in_dim(weights, side * half, half, axis=0)
    mine = swapped(part, "feat", 0)
    other = swapped(mine, "rep", 0)
    low = jnp.where(side == 0, mine, other)
    high = jnp.where(side == 0, other, mine)
    return jnp.concatenate([low, high], axis=0)


def per_device(tokens, cotangent, mix_first, up_weight, down_weight, mix_second, order):
    row_count = tokens.shape[0]
    top_bit = lax.axis_size("feat").bit_length() - 2
    sizes = [row_count * share // sum(SHARES) for share in SHARES]
    offsets = [sum(sizes[:i]) for i in range(len(sizes))]
    cut = lambda x, i: lax.slice_in_dim(x, offsets[i], offsets[i] + sizes[i], axis=0)
    far_in, near_in = [], []
    near_q = neighbour_weights(mix_second[:, 1])
    for i in range(len(sizes)):
        near_in.append(swapped(cut(cotangent, i), "feat", 0))
        far_in.append(swapped(cut(tokens, i), "feat", top_bit))
    grads = None
    backs, directs = [], []
    for i in range(len(sizes)):
        back, direct, grads = process(
            offsets[i], sizes[i], order, tokens, far_in[i], cotangent, near_in[i],
            mix_first, up_weight, down_weight, mix_second, near_q, grads,
        )
        backs.append(swapped(back, "feat", top_bit))
        directs.append(direct)
    first, up, down, second = grads
    second_sum = summed(second, 2)
    near_sum = swapped(second_sum[:, 1].astype(jnp.bfloat16), "feat", 0).astype(jnp.float32)
    second_sum = jnp.stack([second_sum[:, 0], near_sum], axis=1)
    up_sum = summed(up, 1)
    down_sum = summed(down, 1)
    first_sum = summed(first, 2)
    grad_inputs = jnp.concatenate(
        [
            (direct + back.astype(jnp.float32)).astype(jnp.bfloat16)
            for direct, back in zip(directs, backs)
        ],
        axis=0,
    )
    return grad_inputs, first_sum, up_sum, down_sum, second_sum


def solution(mesh):
    placed = (
        P(("groups", "dp", "rep"), "feat"),
        P(("groups", "dp", "rep"), "feat"),
        P("feat", None, None, None),
        P("feat", None, None),
        P("feat", None, None),
        P("feat", None, None, None),
        P("feat"),
    )

    return jax.shard_map(
        per_device,
        mesh=mesh,
        in_specs=placed,
        out_specs=(
            P(("groups", "dp", "rep"), "feat"),
            P(("groups", "feat"), None, ("dp", "rep"), None),
            P(("groups", "feat"), ("dp", "rep"), None),
            P(("groups", "feat"), ("dp", "rep"), None),
            P(("groups", "feat"), None, ("dp", "rep"), None),
        ),
        check_vma=False,
    )
```

```python
import functools

import jax
import jax.numpy as jnp
from jax import lax
from jax.experimental import pallas as pl
from jax.experimental.pallas import tpu as pltpu
from jax.sharding import PartitionSpec as P


GELU_C = 0.7978845608028654
GELU_K = 0.044715
SHARES = (1, 1, 2)


def swapped(x, axis, bit):
    return lax.ppermute(x, axis, [(i, i ^ 1 << bit) for i in range(lax.axis_size(axis))])


def dot(left, right, dims):
    return lax.dot_general(left, right, (dims, ((), ())), preferred_element_type=jnp.float32)


NN = ((1,), (0,))
NT = ((1,), (1,))
TN = ((0,), (0,))


def block_kernel(has_prev, order_ref, x_ref, xf_ref, c_ref, cn_ref, mix_ref, up_ref, down_ref, p_ref, q_ref, *rest):
    if has_prev:
        prev, rest = rest[:4], rest[4:]
    else:
        prev = None
    r_ref, dx_ref, gf_ref, gu_ref, gd_ref, gs_ref = rest
    width = x_ref.shape[1]

    def emit(ref, which, value, index):
        if prev is not None:
            value = value + prev[which][index].astype(jnp.float32)
        ref[index] = value.astype(ref.dtype)

    x2 = jnp.concatenate([x_ref[...], xf_ref[...]], axis=1)
    c2 = jnp.concatenate([c_ref[...], cn_ref[...]], axis=1)
    mix = mix_ref[0].reshape(2 * width, width)
    pq = jnp.concatenate([p_ref[0, 0], q_ref[0]], axis=1)
    up = up_ref[0]
    down = down_ref[0]
    v = dot(x2, mix, NN).astype(jnp.bfloat16)
    dz = dot(c2, pq, NT).astype(jnp.bfloat16)
    h = dot(v, up, NN)
    da = dot(dz, down, NT)
    h2 = h * h
    t = jnp.tanh(h * (GELU_C + (GELU_C * GELU_K) * h2))
    p = 0.5 + 0.5 * t
    act = h * p
    slope = p + act * (1.0 - p) * (2.0 * GELU_C + (6.0 * GELU_C * GELU_K) * h2)
    a = act.astype(jnp.bfloat16)
    dh = (da * slope).astype(jnp.bfloat16)
    z = dot(a, down, NN).astype(jnp.bfloat16)
    du = dot(dh, up, NT).astype(jnp.bfloat16)
    both = dot(du, mix, NT)
    dx_ref[...] = both[:, :width]
    r_ref[...] = both[:, width:].astype(jnp.bfloat16)
    gf = dot(x2, du, TN)
    emit(gf_ref, 0, gf[:width], (0, 0))
    emit(gf_ref, 0, gf[width:], (0, 1))
    emit(gu_ref, 1, dot(v, dh, TN), 0)
    emit(gd_ref, 2, dot(a, dz, TN), 0)
    gs = dot(z, c2, TN)
    emit(gs_ref, 3, gs[:, :width], (0, 0))
    emit(gs_ref, 3, gs[:, width:], (0, 1))


def process(offset, rows, order, tokens, far_in, cotangent, near_in, mix_first, up, down, mix_second, near_q, prev):
    blocks, _, width, _ = mix_first.shape
    hidden = up.shape[2]
    at_source = lambda b, o: (0, o[b])
    act_spec = lambda m: pl.BlockSpec((rows, width), m)
    first_spec = pl.BlockSpec((1, 2, width, width), lambda b, o: (o[b], 0, 0, 0))
    up_spec = pl.BlockSpec((1, width, hidden), lambda b, o: (b, 0, 0))
    down_spec = pl.BlockSpec((1, hidden, width), lambda b, o: (b, 0, 0))
    second_spec = pl.BlockSpec((1, 2, width, width), lambda b, o: (b, 0, 0, 0))
    grad_specs = [first_spec, up_spec, down_spec, second_spec]
    in_specs = [
        act_spec(lambda b, o: (offset // rows, o[b])),
        act_spec(at_source),
        act_spec(lambda b, o: (offset // rows, b)),
        act_spec(lambda b, o: (0, b)),
        first_spec,
        up_spec,
        down_spec,
        pl.BlockSpec((1, 1, width, width), lambda b, o: (b, 0, 0, 0)),
        pl.BlockSpec((1, width, width), lambda b, o: (b, 0, 0)),
    ]
    operands = [tokens, far_in, cotangent, near_in, mix_first, up, down, mix_second, near_q]
    if prev is not None:
        in_specs += grad_specs
        operands += prev
    bf = jnp.bfloat16
    out_shape = [
        jax.ShapeDtypeStruct((rows, blocks * width), bf),
        jax.ShapeDtypeStruct((rows, blocks * width), jnp.float32),
        jax.ShapeDtypeStruct(mix_first.shape, bf),
        jax.ShapeDtypeStruct(up.shape, bf),
        jax.ShapeDtypeStruct(down.shape, bf),
        jax.ShapeDtypeStruct(mix_second.shape, bf),
    ]
    macs = rows * blocks * width * (10 * width + 6 * hidden)
    out = pl.pallas_call(
        functools.partial(block_kernel, prev is not None),
        grid_spec=pltpu.PrefetchScalarGridSpec(
            num_scalar_prefetch=1,
            grid=(blocks,),
            in_specs=in_specs,
            out_specs=[act_spec(at_source), act_spec(at_source)] + grad_specs,
        ),
        out_shape=out_shape,
        compiler_params=pltpu.CompilerParams(dimension_semantics=("arbitrary",)),
        cost_estimate=pl.CostEstimate(
            flops=4 * macs,
            bytes_accessed=60 * 2**20,
            transcendentals=rows * blocks * hidden,
        ),
    )(order, *operands)
    return out[0], out[1], list(out[2:])


def summed(parts, row_dim):
    stages = [("rep", bit) for bit in range(lax.axis_size("rep").bit_length() - 1)]
    dp_bits = lax.axis_size("dp").bit_length() - 1
    rep_bits = len(stages)
    stages += [("dp", bit) for bit in reversed(range(dp_bits))]
    shape = parts.shape
    owners = 1 << (dp_bits + rep_bits)
    names = [("dp", bit) for bit in reversed(range(dp_bits))]
    names += [("rep", bit) for bit in reversed(range(rep_bits))]
    x = parts.reshape(
        shape[:row_dim] + (2,) * len(names) + (shape[row_dim] // owners,) + shape[row_dim + 1 :]
    )
    for axis, bit in stages:
        where = row_dim + names.index((axis, bit))
        names.remove((axis, bit))
        mine = (lax.axis_index(axis) >> bit) & 1
        kept = lax.dynamic_index_in_dim(x, mine, where, keepdims=False)
        sent = lax.dynamic_index_in_dim(x, 1 - mine, where, keepdims=False)
        got = swapped(sent, axis, bit)
        x = kept.astype(jnp.float32) + got.astype(jnp.float32)
        if names:
            x = x.astype(jnp.bfloat16)
    return x


def neighbour_weights(weights):
    quarter = weights.shape[0] // 4
    rep = lax.axis_index("rep") & 1
    dp = lax.axis_index("dp") & 1
    part = lax.dynamic_slice_in_dim(weights, (dp * 2 + rep) * quarter, quarter, axis=0)
    mine = swapped(part, "feat", 0)
    for side, axis in ((rep, "rep"), (dp, "dp")):
        other = swapped(mine, axis, 0)
        low = jnp.where(side == 0, mine, other)
        high = jnp.where(side == 0, other, mine)
        mine = jnp.concatenate([low, high], axis=0)
    return mine


def finish_kernel(direct_ref, back_ref, *rest):
    rest[-1][...] = (direct_ref[...] + back_ref[...].astype(jnp.float32)).astype(jnp.bfloat16)


def finish(offset, total, direct, back, held):
    rows, columns = direct.shape
    tile = rows // 2
    spec = pl.BlockSpec((tile, columns // 4), lambda i, j: (i, j))
    operands = [direct, back]
    in_specs = [spec, spec]
    aliases = {}
    if held is not None:
        operands.append(held)
        in_specs.append(pl.BlockSpec(memory_space=pl.ANY))
        aliases = {2: 0}
    return pl.pallas_call(
        finish_kernel,
        grid=(2, 4),
        in_specs=in_specs,
        out_specs=pl.BlockSpec((tile, columns // 4), lambda i, j: (offset // tile + i, j)),
        out_shape=jax.ShapeDtypeStruct((total, columns), jnp.bfloat16),
        input_output_aliases=aliases,
        cost_estimate=pl.CostEstimate(
            flops=rows * columns, bytes_accessed=8 * rows * columns, transcendentals=0
        ),
    )(*operands)


def per_device(tokens, cotangent, mix_first, up_weight, down_weight, mix_second, order):
    row_count = tokens.shape[0]
    top_bit = lax.axis_size("feat").bit_length() - 2
    sizes = [row_count * share // sum(SHARES) for share in SHARES]
    offsets = [sum(sizes[:i]) for i in range(len(sizes))]
    cut = lambda x, i: lax.slice_in_dim(x, offsets[i], offsets[i] + sizes[i], axis=0)
    far_in, near_in = [], []
    near_q = neighbour_weights(mix_second[:, 1])
    for i in range(len(sizes)):
        near_in.append(swapped(cut(cotangent, i), "feat", 0))
        far_in.append(swapped(cut(tokens, i), "feat", top_bit))
    grads = None
    backs, directs = [], []
    for i in range(len(sizes)):
        back, direct, grads = process(
            offsets[i], sizes[i], order, tokens, far_in[i], cotangent, near_in[i],
            mix_first, up_weight, down_weight, mix_second, near_q, grads,
        )
        backs.append(swapped(back, "feat", top_bit))
        directs.append(direct)
    first, up, down, second = grads
    second_sum = summed(second, 2)
    near_sum = swapped(second_sum[:, 1].astype(jnp.bfloat16), "feat", 0).astype(jnp.float32)
    second_sum = jnp.stack([second_sum[:, 0], near_sum], axis=1)
    up_sum = summed(up, 1)
    down_sum = summed(down, 1)
    first_sum = summed(first, 2)
    grad_inputs = None
    for offset, direct, back in zip(offsets, directs, backs):
        grad_inputs = finish(offset, row_count, direct, back, grad_inputs)
    return grad_inputs, first_sum, up_sum, down_sum, second_sum


def solution(mesh):
    placed = (
        P(("groups", "dp", "rep"), "feat"),
        P(("groups", "dp", "rep"), "feat"),
        P("feat", None, None, None),
        P("feat", None, None),
        P("feat", None, None),
        P("feat", None, None, None),
        P("feat"),
    )

    return jax.shard_map(
        per_device,
        mesh=mesh,
        in_specs=placed,
        out_specs=(
            P(("groups", "dp", "rep"), "feat"),
            P(("groups", "feat"), None, ("dp", "rep"), None),
            P(("groups", "feat"), ("dp", "rep"), None),
            P(("groups", "feat"), ("dp", "rep"), None),
            P(("groups", "feat"), None, ("dp", "rep"), None),
        ),
        check_vma=False,
    )
```
